32 devices in a mesh: grp: 2 (over x), wide: 4 (over y, core), head: 4 (over z).
Axes of the slice: x: 2, y: 2, z: 4, core: 2. Of those that a mesh axis runs over, the one named last changes fastest.
Arguments:
- tokens: bfloat16 [64, 8192], P('grp'), parts along dimension 0, may hold values from -30 to 30
- attn_gain: bfloat16 [8192], replicated, may hold values from 0.25 to 1.75
- ffn_gain: bfloat16 [8192], P('wide'), may hold values from 0.25 to 1.75
- w_query: bfloat16 [8192, 8192], P('wide', 'head'), may hold values from -0.0625 to 0.0625
- key_matrix: bfloat16 [8192, 1024], P('wide', 'head'), may hold values from -0.0625 to 0.0625
- value_matrix: bfloat16 [8192, 1024], P('wide', 'head'), may hold values from -0.0625 to 0.0625
- w_out: bfloat16 [8192, 8192], P('head', 'wide'), may hold values from -0.0625 to 0.0625
- w_gate: bfloat16 [8192, 14336], P('wide', 'head'), may hold values from -0.0625 to 0.0625
- w_up: bfloat16 [8192, 14336], P('wide', 'head'), may hold values from -0.0625 to 0.0625
- w_down: bfloat16 [14336, 8192], P('head', 'wide'), may hold values from -0.046875 to 0.046875
- kv_cache: bfloat16 [2, 16, 2048, 1024], P(None, 'grp', 'wide', 'head'), parts along dimension 1, may hold values from -250 to 250
- lengths: int32 [16], P('grp'), parts along dimension 0, may hold values from 1 to 2048, 8192 in all
- slots: int32 [16], P('grp'), parts along dimension 0, may hold values from 0 to 7, each once
Outputs:
- layer_out: bfloat16 [64, 8192], P(('grp', 'head'), 'wide'), parts along dimension 0
The draws below stay inside these ranges and needn't reach their ends.
There are 2 independent parts, one for each index of `grp`. The reference program is written for one: setup_inputs(seed, part) draws one part's arguments, and reference() takes and returns one part's arrays. A program takes and returns all parts, laid end to end along the dimension named above; an argument that names none is the same for every part. Nothing has to cross between parts.
Inputs may be any that keep to these rules, and one draw needn't show every extreme that they name: `lengths`: they sum to 8192, and the longest is exactly 2048. `slots`: each slot belongs to exactly one request.
All inputs are finite; a program needn't handle non-finite values.
Results may differ from the reference program's by a relative error of at most 0.0057.
Values may be sent and summed in bfloat16 or wider, within the bound.
A program may use at most 128 MiB of HBM per device.

```python
import math
import jax
import jax.numpy as jnp
import numpy as np
from jax import lax

MODEL_WIDTH = 8192
QUERY_HEADS = 64
KEY_HEADS = 8
HEAD_WIDTH = 128
FFW = 14336
DRAFT_TOKENS = 4
GROUP_REQUESTS = 8
CACHE_SLOTS = 2048
TOKENS = 32


def draw_tokens(key, part):
    first_key, key_second_split, key_third_split = jax.random.split(jax.random.fold_in(key, 11), 3)
    column_scale = 10.0 ** (jnp.arange(MODEL_WIDTH, dtype=jnp.float32) / MODEL_WIDTH - 0.4) * jax.random.uniform(first_key, (MODEL_WIDTH,), jnp.float32, 0.8, 1.25)
    row_scale = 10.0 ** jax.random.uniform(key_second_split, (TOKENS, 1), jnp.float32, -0.2, 0.3)
    base = jnp.clip(jax.random.normal(key_third_split, (TOKENS, MODEL_WIDTH), jnp.float32), -3.0, 3.0)
    return (base * row_scale * column_scale[None, :]).astype(jnp.bfloat16)


def draw_kv_cache(key, part):
    first_key = jax.random.fold_in(jax.random.fold_in(key, 23), 0)
    complete_shape = (2, GROUP_REQUESTS, CACHE_SLOTS, KEY_HEADS * HEAD_WIDTH)
    base = jnp.clip(jax.random.normal(first_key, complete_shape, jnp.float32), -4.0, 4.0)
    return base.astype(jnp.bfloat16)


def level_of(key, extent, shards, smallest, top_value):
    factor_of = 1.0
    for axis_at, shards_of in shards:
        draws = jax.random.uniform(jax.random.fold_in(jax.random.fold_in(key, 6), axis_at), (shards_of,), jnp.float32, smallest / len(shards), top_value / len(shards))
        factor_of = factor_of * jnp.repeat(jnp.exp(draws), extent[axis_at] // shards_of).reshape((-1,) + (1,) * (len(extent) - 1 - axis_at))
    return factor_of


def profile(number_of, total, reach, slope):
    weights = [(1 << 20) // math.isqrt(standing ** slope) + 1 for standing in range(2, number_of + 1)]
    spare, holding = total - reach - (number_of - 1), [1] * (number_of - 1)
    while spare > 0:
        candidates = [i for i in range(number_of - 1) if holding[i] < reach]
        mass, left = sum([weights[i] for i in candidates]), spare
        for i in candidates:
            extra = min(reach - holding[i], max(1, left * weights[i] // mass), spare)
            holding[i] = holding[i] + extra
            spare = spare - extra
    return np.array([reach] + holding)


def uneven_parts(rng, number_of, total, bound, skew):
    if number_of == 2:
        one = jax.random.randint(rng, (), max(1, total - bound), min(bound, total - 1) + 1)
        return jnp.stack([one, total - one])
    tallies = jnp.asarray(profile(number_of, total, bound, skew), jnp.int32)
    twos = (number_of - 1) // 2
    giver, sink = tallies[1:1 + 2 * twos:2], tallies[2:2 + 2 * twos:2]
    slack = jnp.minimum(giver - 1, bound - sink)
    shifted = jax.random.randint(jax.random.fold_in(rng, 1), (twos,), 0, 1 << 20) % (slack + 1)
    tallies = tallies.at[1:1 + 2 * twos:2].set(giver - shifted).at[2:2 + 2 * twos:2].set(sink + shifted)
    return tallies[jax.random.permutation(jax.random.fold_in(rng, 2), number_of)]


def gaussian(key, extent, spread, limit, shards=(), kind=jnp.bfloat16):
    drawn = jax.random.normal(key, extent, jnp.float32) * spread
    if len(shards) > 0:
        drawn = level_of(key, extent, shards, -0.22, 0.18) * drawn
    return jnp.clip(drawn, min=-limit, max=limit).astype(kind)


def setup_inputs(seed: int = 0, part: int = 0) -> dict:
    key_list = jax.random.split(jax.random.key(seed), 14)
    part_keys = jax.random.split(jax.random.fold_in(key_list[13], part), 14)
    return {
        "tokens": draw_tokens(jax.random.fold_in(jax.random.fold_in(key_list[13], part), 71), part),
        "attn_gain": jnp.clip(1.0 + 0.15 * jax.random.normal(key_list[1], (MODEL_WIDTH,), jnp.float32), 0.25, 1.75).astype(jnp.bfloat16),
        "ffn_gain": jnp.clip(1.0 + 0.15 * jax.random.normal(key_list[2], (MODEL_WIDTH,), jnp.float32), 0.25, 1.75).astype(jnp.bfloat16),
        "w_query": gaussian(key_list[3], (MODEL_WIDTH, QUERY_HEADS * HEAD_WIDTH), MODEL_WIDTH ** -0.5, 0.0625, ((0, 4), (1, 4))),
        "key_matrix": gaussian(key_list[4], (MODEL_WIDTH, KEY_HEADS * HEAD_WIDTH), MODEL_WIDTH ** -0.5, 0.0625, ((0, 4), (1, 4))),
        "value_matrix": gaussian(key_list[5], (MODEL_WIDTH, KEY_HEADS * HEAD_WIDTH), MODEL_WIDTH ** -0.5, 0.0625, ((0, 4), (1, 4))),
        "w_out": gaussian(key_list[6], (QUERY_HEADS * HEAD_WIDTH, MODEL_WIDTH), (QUERY_HEADS * HEAD_WIDTH) ** -0.5, 0.0625, ((0, 4), (1, 4))),
        "w_gate": gaussian(key_list[7], (MODEL_WIDTH, FFW), MODEL_WIDTH ** -0.5, 0.0625, ((0, 4), (1, 4))),
        "w_up": gaussian(key_list[8], (MODEL_WIDTH, FFW), MODEL_WIDTH ** -0.5, 0.0625, ((0, 4), (1, 4))),
        "w_down": gaussian(key_list[9], (FFW, MODEL_WIDTH), FFW ** -0.5, 0.046875, ((0, 4), (1, 4))),
        "kv_cache": draw_kv_cache(jax.random.fold_in(jax.random.fold_in(key_list[13], part), 71), part),
        "lengths": uneven_parts(part_keys[11], GROUP_REQUESTS, GROUP_REQUESTS * CACHE_SLOTS // 2, CACHE_SLOTS, 2).astype(jnp.int32),
        "slots": jax.random.permutation(part_keys[12], GROUP_REQUESTS).astype(jnp.int32),
    }


epsilon = 1e-05
theta_base = 500000.0
neg_large = -1e+30

def rotary_tables(values, token_positions):
    half_width = values.shape[-1] // 2
    exponent = jnp.arange(half_width, dtype=jnp.float32) * (2.0 / values.shape[-1])
    angles = token_positions[:, None] * (theta_base ** (-exponent))[None, :]
    cosine = jnp.cos(angles)[:, None, :]
    sine_part = jnp.sin(angles)[:, None, :]
    front_half = values[..., :half_width]
    back_half = values[..., half_width:]
    return jnp.concatenate([front_half * cosine - back_half * sine_part, back_half * cosine + front_half * sine_part], axis=-1)

def reference(tokens, attn_gain, ffn_gain, w_query, key_matrix, value_matrix, w_out, w_gate, w_up, w_down, kv_cache, lengths, slots):
    token_row_count = tokens.shape[0]
    tokens_f = tokens.astype(jnp.float32)
    scale_in = lax.rsqrt(lax.optimization_barrier(jnp.mean(tokens_f * tokens_f, axis=1, keepdims=True)) + epsilon)
    normed = (tokens_f * scale_in * attn_gain.astype(jnp.float32)[None, :]).astype(jnp.bfloat16)
    query_sum = jnp.dot(normed, w_query, preferred_element_type=jnp.float32)
    key_total = jnp.dot(normed, key_matrix, preferred_element_type=jnp.float32)
    value_total = jnp.dot(normed, value_matrix, preferred_element_type=jnp.float32)
    token_positions = (jnp.repeat(lengths, DRAFT_TOKENS) + jnp.tile(jnp.arange(DRAFT_TOKENS, dtype=jnp.int32), GROUP_REQUESTS)).astype(jnp.float32)
    rotated_queries = (rotary_tables(query_sum.reshape(token_row_count, QUERY_HEADS, HEAD_WIDTH), token_positions) * HEAD_WIDTH ** (-0.5)).astype(jnp.bfloat16)
    rotated_keys = rotary_tables(key_total.reshape(token_row_count, KEY_HEADS, HEAD_WIDTH), token_positions).astype(jnp.bfloat16)
    fresh_value = value_total.reshape(token_row_count, KEY_HEADS, HEAD_WIDTH).astype(jnp.bfloat16)
    heads_per_group = QUERY_HEADS // KEY_HEADS
    causal = jnp.arange(DRAFT_TOKENS, dtype=jnp.int32)[None, :] <= jnp.arange(DRAFT_TOKENS, dtype=jnp.int32)[:, None]

    def attend(request):
        first_row_index = request * DRAFT_TOKENS
        query_tile_rows = lax.dynamic_slice_in_dim(rotated_queries, first_row_index, DRAFT_TOKENS, 0).reshape(DRAFT_TOKENS, KEY_HEADS, heads_per_group, HEAD_WIDTH).astype(jnp.float32)
        draft_keys = lax.dynamic_slice_in_dim(rotated_keys, first_row_index, DRAFT_TOKENS, 0).astype(jnp.float32)
        draft_vals = lax.dynamic_slice_in_dim(fresh_value, first_row_index, DRAFT_TOKENS, 0).astype(jnp.float32)
        cached_row_index = lax.dynamic_index_in_dim(kv_cache, slots[request], 1, keepdims=False)
        joined_keys = cached_row_index[0].reshape(CACHE_SLOTS, KEY_HEADS, HEAD_WIDTH).astype(jnp.float32)
        joined_values = cached_row_index[1].reshape(CACHE_SLOTS, KEY_HEADS, HEAD_WIDTH).astype(jnp.float32)
        scores = jnp.einsum('jkgd,pkd->kgjp', query_tile_rows, joined_keys)
        live_mask = jnp.arange(CACHE_SLOTS, dtype=jnp.int32) < lengths[request]
        masked = jnp.where(live_mask, scores, neg_large)
        draft_scores = jnp.einsum('jkgd,ikd->kgji', query_tile_rows, draft_keys)
        draft_masked = jnp.where(causal, draft_scores, neg_large)
        top_all = jnp.maximum(lax.optimization_barrier(jnp.max(masked, axis=-1)), lax.optimization_barrier(jnp.max(draft_masked, axis=-1)))
        weights = jnp.where(live_mask, jnp.exp(masked - top_all[..., None]), 0.0)
        draft_weights = jnp.where(causal, jnp.exp(draft_masked - top_all[..., None]), 0.0)
        denominator = lax.optimization_barrier(jnp.sum(weights, axis=-1)) + lax.optimization_barrier(jnp.sum(draft_weights, axis=-1))
        weights_b = lax.optimization_barrier(weights.astype(jnp.bfloat16)).astype(jnp.float32)
        draft_b = lax.optimization_barrier(draft_weights.astype(jnp.bfloat16)).astype(jnp.float32)
        accum = jnp.einsum('kgjp,pkd->kgjd', weights_b, joined_values) + jnp.einsum('kgji,ikd->kgjd', draft_b, draft_vals)
        result = accum / denominator[..., None]
        return result.transpose(2, 0, 1, 3).reshape(DRAFT_TOKENS, QUERY_HEADS * HEAD_WIDTH)
    attended = lax.map(attend, jnp.arange(GROUP_REQUESTS, dtype=jnp.int32)).reshape(token_row_count, QUERY_HEADS * HEAD_WIDTH).astype(jnp.bfloat16)
    resid = (tokens_f + jnp.dot(attended, w_out, preferred_element_type=jnp.float32)).astype(jnp.bfloat16)
    resid_f = resid.astype(jnp.float32)
    scale_mid = lax.rsqrt(lax.optimization_barrier(jnp.mean(resid_f * resid_f, axis=1, keepdims=True)) + epsilon)
    ffn_in = (resid_f * scale_mid * ffn_gain.astype(jnp.float32)[None, :]).astype(jnp.bfloat16)
    gate_sum = jnp.dot(ffn_in, w_gate, preferred_element_type=jnp.float32)
    up_sum = jnp.dot(ffn_in, w_up, preferred_element_type=jnp.float32)
    hidden = (jax.nn.silu(gate_sum) * up_sum).astype(jnp.bfloat16)
    return (resid_f + jnp.dot(hidden, w_down, preferred_element_type=jnp.float32)).astype(jnp.bfloat16)
```

```python
import functools

import jax
import jax.numpy as jnp
from jax import lax
from jax.experimental import pallas as pl
from jax.experimental.pallas import tpu as pltpu
from jax.sharding import PartitionSpec as P

HEAD_WIDTH = 128
DRAFT_TOKENS = 4
SUB = 8
epsilon = 1e-05
theta_base = 500000.0
neg_large = -1e30
F32 = jnp.float32
BF16 = jnp.bfloat16
MESH = pl.DeviceIdType.MESH


def mm(a, b):
    return jnp.dot(a, b, preferred_element_type=F32)


def mm_t(a, b):
    return lax.dot_general(a, b, (((1,), (1,)), ((), ())), preferred_element_type=F32)


def layer_kernel(
    n, nh, cq, co, cg, split,
    slots_ref, lens_ref, tok, gain, fgain, cos, sin,
    wq, wk, wv, wo, wg, wu, wd, cache,
    out,
    wq_v, wk_v, wv_v, wo_v, wg_v, wu_v, wd_v, cache_v,
    x_in, tok_rows, s_q, r_q, s_kv, r_kv, ag_q, qs, ks, vs,
    s_att, r_att, ag_att, x_att, s_o, r_o, ag_r, x_f, s_ss, r_ss,
    s_g, r_g, ag_h, x_h, s_d, r_d,
    sem_wq, sem_w, sem_wg, sem_wd,
    ss_q, rs_q, ss_kv, rs_kv, ss_agq, rs_agq, ss_att, rs_att, ss_aga, rs_aga,
    ss_o, rs_o, ss_agr, rs_agr, ss_ss, rs_ss, ss_g, rs_g, ss_agh, rs_agh, ss_d, rs_d,
):
    me = lax.axis_index("wide")
    hd = lax.axis_index("head")
    total, width = tok.shape
    cols = wq.shape[0]
    qw, kw = wq.shape[1], wk.shape[1]
    ow, fw = wo.shape[1], wg.shape[1]
    kvl = kw // HEAD_WIDTH
    per = qw // kw
    rp, rh = total // n, total // nh
    ctx = cache.shape[2]
    qc, oc, gc = qw // cq, ow // co, fw // cg

    def wq_copy(c):
        at = pl.ds(pl.multiple_of(c * qc, qc), qc)
        return pltpu.make_async_copy(wq.at[:, at], wq_v.at[:, at], sem_wq.at[c])

    def wg_copy(src, dst, j, c):
        at = pl.ds(pl.multiple_of(c * gc, gc), gc)
        return pltpu.make_async_copy(src.at[:, at], dst.at[:, at], sem_wg.at[j, c])

    k_copy = pltpu.make_async_copy(wk, wk_v, sem_w.at[0])
    v_copy = pltpu.make_async_copy(wv, wv_v, sem_w.at[1])
    c_copy = pltpu.make_async_copy(cache, cache_v, sem_w.at[2])
    o_copy = pltpu.make_async_copy(wo, wo_v, sem_w.at[3])
    k_copy.start()
    v_copy.start()
    for c in range(cq):
        wq_copy(c).start()

    barrier = pltpu.get_barrier_semaphore()
    for d in range(1, n):
        pl.semaphore_signal(
            barrier, inc=1, device_id={"wide": lax.rem(me + d, n)}, device_id_type=MESH
        )
    for d in range(1, nh):
        pl.semaphore_signal(
            barrier, inc=1, device_id={"head": lax.rem(hd + d, nh)}, device_id_type=MESH
        )

    def push(axis, mine, size, d, src, dst, ssem, rsem):
        return pltpu.make_async_remote_copy(
            src_ref=src, dst_ref=dst, send_sem=ssem, recv_sem=rsem,
            device_id={axis: lax.rem(mine + d, size)}, device_id_type=MESH,
        )

    def scatter(axis, mine, size, send, recv, ssem, rsem, lead):
        made = []
        for d in range(1, size):
            peer = lax.rem(mine + d, size)
            made.append(
                push(axis, mine, size, d, send.at[lead + (peer,)], recv.at[lead + (d - 1,)],
                     ssem.at[lead + (d - 1,)], rsem.at[lead + (d - 1,)])
            )
        return made

    def gather_start(axis, mine, size, buf, ssem, rsem):
        for d in range(1, size):
            push(axis, mine, size, d, buf.at[mine], buf.at[mine], ssem.at[d - 1],
                 rsem.at[d - 1]).start()

    def gather_wait(axis, mine, size, buf, ssem, rsem):
        for d in range(1, size):
            src = lax.rem(mine + size - d, size)
            push(axis, mine, size, d, buf.at[src], buf.at[src], ssem.at[d - 1],
                 rsem.at[d - 1]).wait_recv()
            push(axis, mine, size, d, buf.at[mine], buf.at[mine], ssem.at[d - 1],
                 rsem.at[d - 1]).wait_send()

    sq = jnp.zeros((total, 1), F32)
    step = width // 8
    for c in range(8):
        part = tok[:, c * step:(c + 1) * step].astype(F32)
        sq = sq + jnp.sum(part * part, axis=1, keepdims=True)
    scale = lax.rsqrt(sq / width + epsilon)
    own = pl.ds(pl.multiple_of(me * cols, cols), cols)
    mine_f = tok[:, own].astype(F32)
    x_in[...] = (mine_f * scale * gain[:, own].astype(F32)).astype(BF16)
    for p in range(nh):
        tok_rows[p] = mine_f[p * rh:(p + 1) * rh]

    k_copy.wait()
    v_copy.wait()
    pl.semaphore_wait(barrier, n - 1 + nh - 1)
    kp = mm(x_in[...], wk_v[...])
    vp = mm(x_in[...], wv_v[...])
    for p in range(n):
        s_kv[p, :, :kw] = kp[p * rp:(p + 1) * rp]
        s_kv[p, :, kw:] = vp[p * rp:(p + 1) * rp]
    for cp in scatter("wide", me, n, s_kv, r_kv, ss_kv, rs_kv, ()):
        cp.start()

    def q_step(c, carry):
        wq_copy(c).wait()
        at = pl.ds(pl.multiple_of(c * qc, qc), qc)
        part = mm(x_in[...], wq_v[:, at])
        for p in range(n):
            s_q[c, p] = part[p * rp:(p + 1) * rp]
        for cp in scatter("wide", me, n, s_q, r_q, ss_q, rs_q, (c,)):
            cp.start()
        return carry

    lax.fori_loop(0, cq, q_step, 0)
    c_copy.start()
    o_copy.start()
    for c in range(cg):
        wg_copy(wg, wg_v, 0, c).start()
        wg_copy(wu, wu_v, 1, c).start()
    if split:
        da_copy = pltpu.make_async_copy(wd.at[:split], wq_v, sem_wd.at[0])
        da_copy.start()
    db_copy = pltpu.make_async_copy(wd.at[split:], wd_v, sem_wd.at[1])
    db_copy.start()

    cos_t, sin_t = cos[me], sin[me]

    def rotate(v):
        return v * cos_t + pltpu.roll(v, HEAD_WIDTH // 2, 1) * sin_t

    for cp in scatter("wide", me, n, s_kv, r_kv, ss_kv, rs_kv, ()):
        cp.wait()
    kv = s_kv[me]
    for d in range(n - 1):
        kv = kv + r_kv[d]
    for h in range(kvl):
        lo = h * HEAD_WIDTH
        ag_q[me, :, qw + lo:qw + lo + HEAD_WIDTH] = rotate(kv[:, lo:lo + HEAD_WIDTH]).astype(BF16)
    ag_q[me, :, qw + kw:] = kv[:, kw:].astype(BF16)
    for c in range(cq):
        for cp in scatter("wide", me, n, s_q, r_q, ss_q, rs_q, (c,)):
            cp.wait()
        qsum = s_q[c, me]
        for d in range(n - 1):
            qsum = qsum + r_q[c, d]
        for h in range(qc // HEAD_WIDTH):
            lo = h * HEAD_WIDTH
            ag_q[me, :, c * qc + lo:c * qc + lo + HEAD_WIDTH] = (
                rotate(qsum[:, lo:lo + HEAD_WIDTH]) * HEAD_WIDTH ** (-0.5)
            ).astype(BF16)
    gather_start("wide", me, n, ag_q, ss_agq, rs_agq)
    c_copy.wait()
    gather_wait("wide", me, n, ag_q, ss_agq, rs_agq)
    for p in range(n):
        rows = ag_q[p].astype(F32)
        at = slice(p * rp, (p + 1) * rp)
        for k in range(kvl):
            for g in range(per):
                lo = (k * per + g) * HEAD_WIDTH
                qs[k, g, at, :] = rows[:, lo:lo + HEAD_WIDTH]
            lo = qw + k * HEAD_WIDTH
            ks[k, at, :] = rows[:, lo:lo + HEAD_WIDTH]
            vs[k, at, :] = rows[:, lo + kw:lo + kw + HEAD_WIDTH]

    pair_rows = per * SUB
    row_of = lax.broadcasted_iota(jnp.int32, (pair_rows, ctx), 0) % SUB
    is_first = row_of < DRAFT_TOKENS
    position = me * ctx + lax.broadcasted_iota(jnp.int32, (pair_rows, ctx), 1)
    d_row = lax.broadcasted_iota(jnp.int32, (pair_rows, total), 0) % SUB
    d_col = lax.broadcasted_iota(jnp.int32, (pair_rows, total), 1)
    lane = lax.broadcasted_iota(jnp.int32, (SUB, HEAD_WIDTH), 1)
    chief = jnp.where(me == 0, 0, 1 << 20)

    def attend(t, carry):
        slot0, slot1 = slots_ref[2 * t], slots_ref[2 * t + 1]
        bound = jnp.where(is_first, lens_ref[2 * t], lens_ref[2 * t + 1])
        live = position < bound
        own_row = d_row + t * SUB
        d_live = (
            (d_col // DRAFT_TOKENS == own_row // DRAFT_TOKENS)
            & (d_col <= own_row)
            & (d_col >= chief)
        )
        for k in range(kvl):
            at = slice(k * HEAD_WIDTH, (k + 1) * HEAD_WIDTH)
            q = qs[k, :, pl.ds(pl.multiple_of(t * SUB, SUB), SUB), :]
            q = q.reshape(pair_rows, HEAD_WIDTH).astype(BF16)
            sc = jnp.where(
                is_first, mm_t(q, cache_v[0, slot0, :, at]), mm_t(q, cache_v[0, slot1, :, at])
            )
            sc = jnp.where(live, sc, neg_large)
            sd = jnp.where(d_live, mm_t(q, ks[k].astype(BF16)), neg_large)
            top = jnp.maximum(
                jnp.max(sc, axis=1, keepdims=True), jnp.max(sd, axis=1, keepdims=True)
            )
            w = jnp.where(live, jnp.exp(sc - top), 0.0)
            u = jnp.where(d_live, jnp.exp(sd - top), 0.0)
            den = jnp.sum(w, axis=1, keepdims=True) + jnp.sum(u, axis=1, keepdims=True)
            acc = (
                mm(jnp.where(is_first, w, 0.0).astype(BF16), cache_v[1, slot0, :, at])
                + mm(jnp.where(is_first, 0.0, w).astype(BF16), cache_v[1, slot1, :, at])
                + mm(u.astype(BF16), vs[k].astype(BF16))
            )
            acc = acc.reshape(per, SUB, HEAD_WIDTH)
            packed = jnp.zeros((SUB, HEAD_WIDTH), F32)
            for g in range(per):
                rows = slice(g * SUB, (g + 1) * SUB)
                packed = jnp.where(lane == g, top[rows], packed)
                packed = jnp.where(lane == per + g, den[rows], packed)
            for o in range(SUB // rp):
                at_p = t * (SUB // rp) + o
                rows = slice(o * rp, (o + 1) * rp)
                for g in range(per):
                    s_att[at_p, k, g] = acc[g, rows]
                s_att[at_p, k, per] = packed[rows]
        return carry

    lax.fori_loop(0, total // SUB, attend, 0)
    att_moves = scatter("wide", me, n, s_att, r_att, ss_att, rs_att, ())
    for cp in att_moves:
        cp.start()
    for cp in att_moves:
        cp.wait()
    for k in range(kvl):
        stats = [s_att[me, k, per]] + [r_att[d, k, per] for d in range(n - 1)]
        top = stats[0]
        for st in stats[1:]:
            top = jnp.maximum(top, st)
        shrink = [jnp.exp(st - top) for st in stats]
        for g in range(per):
            num = jnp.zeros((rp, HEAD_WIDTH), F32)
            den = jnp.zeros((rp, 1), F32)
            for i in range(n):
                f = shrink[i][:, g:g + 1]
                part = s_att[me, k, g] if i == 0 else r_att[i - 1, k, g]
                num = num + f * part
                den = den + f * stats[i][:, per + g:per + g + 1]
            lo = (k * per + g) * HEAD_WIDTH
            ag_att[me, :, lo:lo + HEAD_WIDTH] = (num / den).astype(BF16)
    gather_start("wide", me, n, ag_att, ss_aga, rs_aga)
    o_copy.wait()
    gather_wait("wide", me, n, ag_att, ss_aga, rs_aga)
    x_att[...] = jnp.concatenate([ag_att[p].astype(F32) for p in range(n)], axis=0).astype(BF16)

    def o_step(c, carry):
        at = pl.ds(pl.multiple_of(c * oc, oc), oc)
        part = mm(x_att[...], wo_v[:, at])
        for p in range(nh):
            s_o[c, p] = part[p * rh:(p + 1) * rh]
        for cp in scatter("head", hd, nh, s_o, r_o, ss_o, rs_o, (c,)):
            cp.start()
        return carry

    lax.fori_loop(0, co, o_step, 0)
    for c in range(co):
        for cp in scatter("head", hd, nh, s_o, r_o, ss_o, rs_o, (c,)):
            cp.wait()
        osum = s_o[c, hd]
        for d in range(nh - 1):
            osum = osum + r_o[c, d]
        at = slice(c * oc, (c + 1) * oc)
        ag_r[hd, :, at] = (tok_rows[hd, :, at] + osum).astype(BF16)
    gather_start("head", hd, nh, ag_r, ss_agr, rs_agr)
    gather_wait("head", hd, nh, ag_r, ss_agr, rs_agr)
    resid = jnp.concatenate([ag_r[p].astype(F32) for p in range(nh)], axis=0)
    x_f[...] = (resid * fgain[...].astype(F32)).astype(BF16)
    squares = jnp.broadcast_to(jnp.sum(resid * resid, axis=1, keepdims=True), (total, HEAD_WIDTH))
    for p in range(n):
        s_ss[p] = squares[p * rp:(p + 1) * rp]
    ss_moves = scatter("wide", me, n, s_ss, r_ss, ss_ss, rs_ss, ())
    for cp in ss_moves:
        cp.start()

    def g_step(c, carry):
        wg_copy(wg, wg_v, 0, c).wait()
        wg_copy(wu, wu_v, 1, c).wait()
        at = pl.ds(pl.multiple_of(c * gc, gc), gc)
        gate = mm(x_f[...], wg_v[:, at])
        up = mm(x_f[...], wu_v[:, at])
        for p in range(n):
            s_g[c, p, 0] = gate[p * rp:(p + 1) * rp]
            s_g[c, p, 1] = up[p * rp:(p + 1) * rp]
        for cp in scatter("wide", me, n, s_g, r_g, ss_g, rs_g, (c,)):
            cp.start()
        return carry

    lax.fori_loop(0, cg, g_step, 0)
    for cp in ss_moves:
        cp.wait()
    sq = s_ss[me]
    for d in range(n - 1):
        sq = sq + r_ss[d]
    scale = lax.rsqrt(sq[:, :1] / width + epsilon)
    for c in range(cg):
        for cp in scatter("wide", me, n, s_g, r_g, ss_g, rs_g, (c,)):
            cp.wait()
        gate, up = s_g[c, me, 0], s_g[c, me, 1]
        for d in range(n - 1):
            gate = gate + r_g[c, d, 0]
            up = up + r_g[c, d, 1]
        gate = gate * scale
        up = up * scale
        ag_h[me, :, c * gc:(c + 1) * gc] = (gate / (1.0 + jnp.exp(-gate)) * up).astype(BF16)
    gather_start("wide", me, n, ag_h, ss_agh, rs_agh)
    if split:
        da_copy.wait()
    db_copy.wait()
    gather_wait("wide", me, n, ag_h, ss_agh, rs_agh)
    x_h[...] = jnp.concatenate([ag_h[p].astype(F32) for p in range(n)], axis=0).astype(BF16)

    def d_step(c, carry):
        at = pl.ds(pl.multiple_of(c * oc, oc), oc)
        part = mm(x_h[:, split:], wd_v[:, at])
        if split:
            part = part + mm(x_h[:, :split], wq_v[:, at])
        for p in range(nh):
            s_d[c, p] = part[p * rh:(p + 1) * rh]
        for cp in scatter("head", hd, nh, s_d, r_d, ss_d, rs_d, (c,)):
            cp.start()
        return carry

    lax.fori_loop(0, co, d_step, 0)
    for c in range(co):
        for cp in scatter("head", hd, nh, s_d, r_d, ss_d, rs_d, (c,)):
            cp.wait()
        dsum = s_d[c, hd]
        for d in range(nh - 1):
            dsum = dsum + r_d[c, d]
        at = slice(c * oc, (c + 1) * oc)
        out[:, at] = (ag_r[hd, :, at].astype(F32) + dsum).astype(BF16)


def chunks_of(columns, wanted, peers):
    if peers > 4 or columns % (wanted * HEAD_WIDTH):
        return 1
    return wanted


def per_device(
    n, nh,
    tokens, attn_gain, ffn_gain, w_query, key_matrix, value_matrix,
    w_out, w_gate, w_up, w_down, kv_cache, lengths, slots,
):
    total, width = tokens.shape
    cols, qw = w_query.shape
    kw = key_matrix.shape[1]
    ow, fw = w_out.shape[1], w_gate.shape[1]
    kvl, per = kw // HEAD_WIDTH, qw // kw
    rp, rh = total // n, total // nh
    cq, co = chunks_of(qw, 4, n), chunks_of(ow, 4, nh)
    cg = chunks_of(fw, 7, n)
    qc, oc, gc = qw // cq, ow // co, fw // cg
    split = cols if w_down.shape[1] == qw and w_down.shape[0] > cols else 0
    positions = (
        jnp.repeat(lengths, DRAFT_TOKENS) + jnp.arange(total, dtype=jnp.int32) % DRAFT_TOKENS
    ).astype(F32)
    exponent = jnp.arange(HEAD_WIDTH // 2, dtype=F32) * (2.0 / HEAD_WIDTH)
    angles = positions[:, None] * (theta_base ** (-exponent))[None, :]
    cosine, sine = jnp.cos(angles), jnp.sin(angles)
    cos2 = jnp.concatenate([cosine, cosine], axis=1).reshape(n, rp, HEAD_WIDTH)
    sin2 = jnp.concatenate([-sine, sine], axis=1).reshape(n, rp, HEAD_WIDTH)
    vmem = pl.BlockSpec(memory_space=pltpu.VMEM)
    smem = pl.BlockSpec(memory_space=pltpu.SMEM)
    hbm = pl.BlockSpec(memory_space=pl.ANY)
    V = pltpu.VMEM

    def sems(*shape):
        return [pltpu.SemaphoreType.DMA(shape)] * 2

    scratch = [
        V(w_query.shape, BF16), V(key_matrix.shape, BF16), V(value_matrix.shape, BF16),
        V(w_out.shape, BF16), V(w_gate.shape, BF16), V(w_up.shape, BF16),
        V((w_down.shape[0] - split, w_down.shape[1]), BF16), V(kv_cache.shape, BF16),
        V((total, cols), BF16), V((nh, rh, cols), F32),
        V((cq, n, rp, qc), F32), V((cq, n - 1, rp, qc), F32),
        V((n, rp, 2 * kw), F32), V((n - 1, rp, 2 * kw), F32),
        V((n, rp, qw + 2 * kw), BF16),
        V((kvl, per, total, HEAD_WIDTH), F32),
        V((kvl, total, HEAD_WIDTH), F32), V((kvl, total, HEAD_WIDTH), F32),
        V((n, kvl, per + 1, rp, HEAD_WIDTH), F32), V((n - 1, kvl, per + 1, rp, HEAD_WIDTH), F32),
        V((n, rp, qw), BF16), V((total, qw), BF16),
        V((co, nh, rh, oc), F32), V((co, nh - 1, rh, oc), F32),
        V((nh, rh, ow), BF16), V((total, ow), BF16),
        V((n, rp, HEAD_WIDTH), F32), V((n - 1, rp, HEAD_WIDTH), F32),
        V((cg, n, 2, rp, gc), F32), V((cg, n - 1, 2, rp, gc), F32),
        V((n, rp, fw), BF16), V((total, fw), BF16),
        V((co, nh, rh, oc), F32), V((co, nh - 1, rh, oc), F32),
        pltpu.SemaphoreType.DMA((cq,)), pltpu.SemaphoreType.DMA((4,)),
        pltpu.SemaphoreType.DMA((2, cg)), pltpu.SemaphoreType.DMA((2,)),
        *sems(cq, n - 1), *sems(n - 1), *sems(n - 1), *sems(n - 1), *sems(n - 1),
        *sems(co, nh - 1), *sems(nh - 1), *sems(n - 1), *sems(cg, n - 1),
        *sems(n - 1), *sems(co, nh - 1),
    ]
    return pl.pallas_call(
        functools.partial(layer_kernel, n, nh, cq, co, cg, split),
        out_shape=jax.ShapeDtypeStruct((rh, ow), BF16),
        in_specs=[smem, smem] + [vmem] * 5 + [hbm] * 8,
        out_specs=vmem,
        scratch_shapes=scratch,
        compiler_params=pltpu.CompilerParams(
            collective_id=0, has_side_effects=True, vmem_limit_bytes=67043328
        ),
    )(
        slots, lengths, tokens, attn_gain[None, :], ffn_gain[None, :], cos2, sin2,
        w_query, key_matrix, value_matrix, w_out, w_gate, w_up, w_down, kv_cache,
    )


def solution(mesh):
    in_specs = (
        P("grp", None),
        P(),
        P("wide"),
        P("wide", "head"),
        P("wide", "head"),
        P("wide", "head"),
        P("head", "wide"),
        P("wide", "head"),
        P("wide", "head"),
        P("head", "wide"),
        P(None, "grp", "wide", "head"),
        P("grp"),
        P("grp"),
    )
    return jax.shard_map(
        functools.partial(per_device, mesh.shape["wide"], mesh.shape["head"]),
        mesh=mesh, in_specs=in_specs, out_specs=P(("grp", "head"), "wide"), check_vma=False,
    )
```

```python
import functools

import jax
import jax.numpy as jnp
from jax import lax
from jax.experimental import pallas as pl
from jax.experimental.pallas import tpu as pltpu
from jax.sharding import PartitionSpec as P

HEAD_WIDTH = 128
DRAFT_TOKENS = 4
SUB = 8
LAG = 2
epsilon = 1e-05
theta_base = 500000.0
neg_large = -1e30
F32 = jnp.float32
BF16 = jnp.bfloat16
MESH = pl.DeviceIdType.MESH


def mm(a, b):
    return jnp.dot(a, b, preferred_element_type=F32)


def mm_t(a, b):
    return lax.dot_general(a, b, (((1,), (1,)), ((), ())), preferred_element_type=F32)


def layer_kernel(
    n, nh, cq, co, cg, split,
    slots_ref, lens_ref, tok, gain, fgain, cos, sin,
    wq, wk, wv, wo, wg, wu, wd, cache,
    out,
    wq_v, wk_v, wv_v, wo_v, wg_v, wu_v, wd_v, cache_v,
    x_in, tok_rows, s_q, r_q, s_kv, r_kv, ag_q, ag_kv, qs, ks, vs,
    s_att, r_att, ag_att, x_att, s_o, r_o, ag_r, x_f, s_ss, r_ss, row_scale,
    s_g, r_g, ag_h, x_h, s_d, r_d,
    sem_wq, sem_w, sem_wg, sem_wd,
    ss_q, rs_q, ss_kv, rs_kv, ss_agq, rs_agq, ss_agkv, rs_agkv, ss_att, rs_att, ss_aga, rs_aga,
    ss_o, rs_o, ss_agr, rs_agr, ss_ss, rs_ss, ss_g, rs_g, ss_agh, rs_agh, ss_d, rs_d,
):
    me = lax.axis_index("wide")
    hd = lax.axis_index("head")
    total, width = tok.shape
    cols = wq.shape[0]
    qw, kw = wq.shape[1], wk.shape[1]
    ow, fw = wo.shape[1], wg.shape[1]
    kvl = kw // HEAD_WIDTH
    per = qw // kw
    rp, rh = total // n, total // nh
    ctx = cache.shape[2]
    qc, oc, gc = qw // cq, ow // co, fw // cg

    def wq_copy(c):
        at = pl.ds(pl.multiple_of(c * qc, qc), qc)
        return pltpu.make_async_copy(wq.at[:, at], wq_v.at[:, at], sem_wq.at[c])

    def wg_copy(src, dst, j, c):
        at = pl.ds(pl.multiple_of(c * gc, gc), gc)
        return pltpu.make_async_copy(src.at[:, at], dst.at[:, at], sem_wg.at[j, c])

    k_copy = pltpu.make_async_copy(wk, wk_v, sem_w.at[0])
    v_copy = pltpu.make_async_copy(wv, wv_v, sem_w.at[1])
    c_copy = pltpu.make_async_copy(cache, cache_v, sem_w.at[2])
    o_copy = pltpu.make_async_copy(wo, wo_v, sem_w.at[3])
    k_copy.start()
    v_copy.start()
    for c in range(cq):
        wq_copy(c).start()

    barrier = pltpu.get_barrier_semaphore()
    for d in range(1, n):
        pl.semaphore_signal(
            barrier, inc=1, device_id={"wide": lax.rem(me + d, n)}, device_id_type=MESH
        )
    for d in range(1, nh):
        pl.semaphore_signal(
            barrier, inc=1, device_id={"head": lax.rem(hd + d, nh)}, device_id_type=MESH
        )

    def push(axis, mine, size, d, src, dst, ssem, rsem):
        return pltpu.make_async_remote_copy(
            src_ref=src, dst_ref=dst, send_sem=ssem, recv_sem=rsem,
            device_id={axis: lax.rem(mine + d, size)}, device_id_type=MESH,
        )

    def scatter(axis, mine, size, send, recv, ssem, rsem, lead):
        made = []
        for d in range(1, size):
            peer = lax.rem(mine + d, size)
            made.append(
                push(axis, mine, size, d, send.at[lead + (peer,)], recv.at[lead + (d - 1,)],
                     ssem.at[lead + (d - 1,)], rsem.at[lead + (d - 1,)])
            )
        return made

    def gather_start(axis, mine, size, buf, ssem, rsem, lead=()):
        for d in range(1, size):
            own_at, sem_at = lead + (mine,), lead + (d - 1,)
            push(axis, mine, size, d, buf.at[own_at], buf.at[own_at], ssem.at[sem_at],
                 rsem.at[sem_at]).start()

    def gather_wait(axis, mine, size, buf, ssem, rsem, lead=()):
        for d in range(1, size):
            own_at, sem_at = lead + (mine,), lead + (d - 1,)
            src_at = lead + (lax.rem(mine + size - d, size),)
            push(axis, mine, size, d, buf.at[src_at], buf.at[src_at], ssem.at[sem_at],
                 rsem.at[sem_at]).wait_recv()
            push(axis, mine, size, d, buf.at[own_at], buf.at[own_at], ssem.at[sem_at],
                 rsem.at[sem_at]).wait_send()

    def staged(count, produce, settle, between=None):
        lag = min(LAG, count)

        def first(c, carry):
            produce(c)
            return carry

        def both(c, carry):
            produce(c)
            settle(c - lag)
            return carry

        lax.fori_loop(0, lag, first, 0)
        if between is not None:
            between()
        if count > lag:
            lax.fori_loop(lag, count, both, 0)
        for c in range(count - lag, count):
            settle(c)

    sq = jnp.zeros((total, 1), F32)
    step = width // 8
    for c in range(8):
        part = tok[:, c * step:(c + 1) * step].astype(F32)
        sq = sq + jnp.sum(part * part, axis=1, keepdims=True)
    scale = lax.rsqrt(sq / width + epsilon)
    own = pl.ds(pl.multiple_of(me * cols, cols), cols)
    mine_f = tok[:, own].astype(F32)
    x_in[...] = (mine_f * scale * gain[:, own]).astype(BF16)
    for p in range(nh):
        tok_rows[p] = mine_f[p * rh:(p + 1) * rh]

    k_copy.wait()
    v_copy.wait()
    pl.semaphore_wait(barrier, n - 1 + nh - 1)
    kp = mm(x_in[...], wk_v[...])
    vp = mm(x_in[...], wv_v[...])
    for p in range(n):
        s_kv[p, :, :kw] = kp[p * rp:(p + 1) * rp]
        s_kv[p, :, kw:] = vp[p * rp:(p + 1) * rp]
    for cp in scatter("wide", me, n, s_kv, r_kv, ss_kv, rs_kv, ()):
        cp.start()

    cos_t, sin_t = cos[me], sin[me]

    def rotate(v):
        return v * cos_t + pltpu.roll(v, HEAD_WIDTH // 2, 1) * sin_t

    def q_step(c):
        wq_copy(c).wait()
        at = pl.ds(pl.multiple_of(c * qc, qc), qc)
        part = mm(x_in[...], wq_v[:, at])
        for p in range(n):
            s_q[c, p] = part[p * rp:(p + 1) * rp]
        for cp in scatter("wide", me, n, s_q, r_q, ss_q, rs_q, (c,)):
            cp.start()

    def q_settle(c):
        for cp in scatter("wide", me, n, s_q, r_q, ss_q, rs_q, (c,)):
            cp.wait()
        qsum = s_q[c, me]
        for d in range(n - 1):
            qsum = qsum + r_q[c, d]
        for h in range(qc // HEAD_WIDTH):
            lo = h * HEAD_WIDTH
            ag_q[c, me, :, lo:lo + HEAD_WIDTH] = (
                rotate(qsum[:, lo:lo + HEAD_WIDTH]) * HEAD_WIDTH ** (-0.5)
            ).astype(BF16)
        gather_start("wide", me, n, ag_q, ss_agq, rs_agq, (c,))

    def kv_settle():
        for cp in scatter("wide", me, n, s_kv, r_kv, ss_kv, rs_kv, ()):
            cp.wait()
        kv = s_kv[me]
        for d in range(n - 1):
            kv = kv + r_kv[d]
        for h in range(kvl):
            lo = h * HEAD_WIDTH
            ag_kv[me, :, lo:lo + HEAD_WIDTH] = rotate(kv[:, lo:lo + HEAD_WIDTH]).astype(BF16)
        ag_kv[me, :, kw:] = kv[:, kw:].astype(BF16)
        gather_start("wide", me, n, ag_kv, ss_agkv, rs_agkv)
        c_copy.start()
        o_copy.start()
        for c in range(cg):
            wg_copy(wg, wg_v, 0, c).start()
            wg_copy(wu, wu_v, 1, c).start()
        db_copy.start()

    db_copy = pltpu.make_async_copy(wd.at[split:], wd_v, sem_wd.at[1])
    staged(cq, q_step, q_settle, kv_settle)
    if split:
        da_copy = pltpu.make_async_copy(wd.at[:split], wq_v, sem_wd.at[0])
        da_copy.start()
    c_copy.wait()
    gather_wait("wide", me, n, ag_kv, ss_agkv, rs_agkv)
    for c in range(cq):
        gather_wait("wide", me, n, ag_q, ss_agq, rs_agq, (c,))
    for p in range(n):
        at = slice(p * rp, (p + 1) * rp)
        for h in range(kvl * per):
            c, lo = divmod(h * HEAD_WIDTH, qc)
            qs[h // per, h % per, at, :] = ag_q[c, p, :, lo:lo + HEAD_WIDTH].astype(F32)
        rows = ag_kv[p].astype(F32)
        for k in range(kvl):
            lo = k * HEAD_WIDTH
            ks[k, at, :] = rows[:, lo:lo + HEAD_WIDTH]
            vs[k, at, :] = rows[:, lo + kw:lo + kw + HEAD_WIDTH]

    pair_rows = per * SUB
    row_of = lax.broadcasted_iota(jnp.int32, (pair_rows, ctx), 0) % SUB
    is_first = row_of < DRAFT_TOKENS
    position = me * ctx + lax.broadcasted_iota(jnp.int32, (pair_rows, ctx), 1)
    d_row = lax.broadcasted_iota(jnp.int32, (pair_rows, total), 0) % SUB
    d_col = lax.broadcasted_iota(jnp.int32, (pair_rows, total), 1)
    lane = lax.broadcasted_iota(jnp.int32, (SUB, HEAD_WIDTH), 1)
    chief = jnp.where(me == 0, 0, 1 << 20)

    def attend(t, carry):
        slot0, slot1 = slots_ref[2 * t], slots_ref[2 * t + 1]
        bound = jnp.where(is_first, lens_ref[2 * t], lens_ref[2 * t + 1])
        live = position < bound
        own_row = d_row + t * SUB
        d_live = (
            (d_col // DRAFT_TOKENS == own_row // DRAFT_TOKENS)
            & (d_col <= own_row)
            & (d_col >= chief)
        )
        for k in range(kvl):
            at = slice(k * HEAD_WIDTH, (k + 1) * HEAD_WIDTH)
            q = qs[k, :, pl.ds(pl.multiple_of(t * SUB, SUB), SUB), :]
            q = q.reshape(pair_rows, HEAD_WIDTH).astype(BF16)
            sc = jnp.where(
                is_first, mm_t(q, cache_v[0, slot0, :, at]), mm_t(q, cache_v[0, slot1, :, at])
            )
            sc = jnp.where(live, sc, neg_large)
            sd = jnp.where(d_live, mm_t(q, ks[k].astype(BF16)), neg_large)
            top = jnp.maximum(
                jnp.max(sc, axis=1, keepdims=True), jnp.max(sd, axis=1, keepdims=True)
            )
            w = jnp.where(live, jnp.exp(sc - top), 0.0)
            u = jnp.where(d_live, jnp.exp(sd - top), 0.0)
            den = jnp.sum(w, axis=1, keepdims=True) + jnp.sum(u, axis=1, keepdims=True)
            acc = (
                mm(jnp.where(is_first, w, 0.0).astype(BF16), cache_v[1, slot0, :, at])
                + mm(jnp.where(is_first, 0.0, w).astype(BF16), cache_v[1, slot1, :, at])
                + mm(u.astype(BF16), vs[k].astype(BF16))
            )
            acc = acc.reshape(per, SUB, HEAD_WIDTH)
            packed = jnp.zeros((SUB, HEAD_WIDTH), F32)
            for g in range(per):
                rows = slice(g * SUB, (g + 1) * SUB)
                packed = jnp.where(lane == g, top[rows], packed)
                packed = jnp.where(lane == per + g, den[rows], packed)
            for o in range(SUB // rp):
                at_p = t * (SUB // rp) + o
                rows = slice(o * rp, (o + 1) * rp)
                for g in range(per):
                    s_att[at_p, k, g] = acc[g, rows]
                s_att[at_p, k, per] = packed[rows]
        return carry

    lax.fori_loop(0, total // SUB, attend, 0)
    att_moves = scatter("wide", me, n, s_att, r_att, ss_att, rs_att, ())
    for cp in att_moves:
        cp.start()
    for cp in att_moves:
        cp.wait()
    for k in range(kvl):
        stats = [s_att[me, k, per]] + [r_att[d, k, per] for d in range(n - 1)]
        top = stats[0]
        for st in stats[1:]:
            top = jnp.maximum(top, st)
        shrink = [jnp.exp(st - top) for st in stats]
        for g in range(per):
            num = jnp.zeros((rp, HEAD_WIDTH), F32)
            den = jnp.zeros((rp, 1), F32)
            for i in range(n):
                f = shrink[i][:, g:g + 1]
                part = s_att[me, k, g] if i == 0 else r_att[i - 1, k, g]
                num = num + f * part
                den = den + f * stats[i][:, per + g:per + g + 1]
            lo = (k * per + g) * HEAD_WIDTH
            ag_att[me, :, lo:lo + HEAD_WIDTH] = (num / den).astype(BF16)
    gather_start("wide", me, n, ag_att, ss_aga, rs_aga)
    o_copy.wait()
    gather_wait("wide", me, n, ag_att, ss_aga, rs_aga)
    x_att[...] = jnp.concatenate([ag_att[p].astype(F32) for p in range(n)], axis=0).astype(BF16)

    def o_step(c):
        at = pl.ds(pl.multiple_of(c * oc, oc), oc)
        part = mm(x_att[...], wo_v[:, at])
        for p in range(nh):
            s_o[c, p] = part[p * rh:(p + 1) * rh]
        for cp in scatter("head", hd, nh, s_o, r_o, ss_o, rs_o, (c,)):
            cp.start()

    def o_settle(c):
        for cp in scatter("head", hd, nh, s_o, r_o, ss_o, rs_o, (c,)):
            cp.wait()
        osum = s_o[c, hd]
        for d in range(nh - 1):
            osum = osum + r_o[c, d]
        at = pl.ds(pl.multiple_of(c * oc, oc), oc)
        ag_r[c, hd] = (tok_rows[hd, :, at] + osum).astype(BF16)
        gather_start("head", hd, nh, ag_r, ss_agr, rs_agr, (c,))

    staged(co, o_step, o_settle)
    square = jnp.zeros((total, 1), F32)
    for c in range(co):
        gather_wait("head", hd, nh, ag_r, ss_agr, rs_agr, (c,))
        resid = jnp.concatenate([ag_r[c, p].astype(F32) for p in range(nh)], axis=0)
        at = slice(c * oc, (c + 1) * oc)
        x_f[:, at] = (resid * fgain[:, at]).astype(BF16)
        square = square + jnp.sum(resid * resid, axis=1, keepdims=True)
    squares = jnp.broadcast_to(square, (total, HEAD_WIDTH))
    for p in range(n):
        s_ss[p] = squares[p * rp:(p + 1) * rp]
    ss_moves = scatter("wide", me, n, s_ss, r_ss, ss_ss, rs_ss, ())
    for cp in ss_moves:
        cp.start()

    def g_step(c):
        wg_copy(wg, wg_v, 0, c).wait()
        wg_copy(wu, wu_v, 1, c).wait()
        at = pl.ds(pl.multiple_of(c * gc, gc), gc)
        gate = mm(x_f[...], wg_v[:, at])
        up = mm(x_f[...], wu_v[:, at])
        for p in range(n):
            s_g[c, p, 0] = gate[p * rp:(p + 1) * rp]
            s_g[c, p, 1] = up[p * rp:(p + 1) * rp]
        for cp in scatter("wide", me, n, s_g, r_g, ss_g, rs_g, (c,)):
            cp.start()

    def ss_settle():
        for cp in ss_moves:
            cp.wait()
        sq = s_ss[me]
        for d in range(n - 1):
            sq = sq + r_ss[d]
        row_scale[...] = lax.rsqrt(sq / width + epsilon)

    def g_settle(c):
        for cp in scatter("wide", me, n, s_g, r_g, ss_g, rs_g, (c,)):
            cp.wait()
        gate, up = s_g[c, me, 0], s_g[c, me, 1]
        for d in range(n - 1):
            gate = gate + r_g[c, d, 0]
            up = up + r_g[c, d, 1]
        scale = row_scale[...][:, :1]
        gate = gate * scale
        up = up * scale
        ag_h[c, me] = (gate / (1.0 + jnp.exp(-gate)) * up).astype(BF16)
        gather_start("wide", me, n, ag_h, ss_agh, rs_agh, (c,))

    staged(cg, g_step, g_settle, ss_settle)
    if split:
        da_copy.wait()
    db_copy.wait()
    for c in range(cg):
        gather_wait("wide", me, n, ag_h, ss_agh, rs_agh, (c,))
        x_h[:, c * gc:(c + 1) * gc] = jnp.concatenate(
            [ag_h[c, p].astype(F32) for p in range(n)], axis=0
        ).astype(BF16)

    def d_step(c):
        at = pl.ds(pl.multiple_of(c * oc, oc), oc)
        part = mm(x_h[:, split:], wd_v[:, at])
        if split:
            part = part + mm(x_h[:, :split], wq_v[:, at])
        for p in range(nh):
            s_d[c, p] = part[p * rh:(p + 1) * rh]
        for cp in scatter("head", hd, nh, s_d, r_d, ss_d, rs_d, (c,)):
            cp.start()

    def d_settle(c):
        for cp in scatter("head", hd, nh, s_d, r_d, ss_d, rs_d, (c,)):
            cp.wait()
        dsum = s_d[c, hd]
        for d in range(nh - 1):
            dsum = dsum + r_d[c, d]
        at = pl.ds(pl.multiple_of(c * oc, oc), oc)
        out[:, at] = (ag_r[c, hd].astype(F32) + dsum).astype(BF16)

    staged(co, d_step, d_settle)


def chunks_of(columns, wanted, peers):
    if peers > 4 or columns % (wanted * HEAD_WIDTH):
        return 1
    return wanted


def per_device(
    n, nh,
    tokens, attn_gain, ffn_gain, w_query, key_matrix, value_matrix,
    w_out, w_gate, w_up, w_down, kv_cache, lengths, slots,
):
    total, width = tokens.shape
    cols, qw = w_query.shape
    kw = key_matrix.shape[1]
    ow, fw = w_out.shape[1], w_gate.shape[1]
    kvl, per = kw // HEAD_WIDTH, qw // kw
    rp, rh = total // n, total // nh
    cq, co = chunks_of(qw, 4, n), chunks_of(ow, 4, nh)
    cg = chunks_of(fw, 7, n)
    qc, oc, gc = qw // cq, ow // co, fw // cg
    split = cols if w_down.shape[1] == qw and w_down.shape[0] > cols else 0
    positions = (
        jnp.repeat(lengths, DRAFT_TOKENS) + jnp.arange(total, dtype=jnp.int32) % DRAFT_TOKENS
    ).astype(F32)
    exponent = jnp.arange(HEAD_WIDTH // 2, dtype=F32) * (2.0 / HEAD_WIDTH)
    angles = positions[:, None] * (theta_base ** (-exponent))[None, :]
    cosine, sine = jnp.cos(angles), jnp.sin(angles)
    cos2 = jnp.concatenate([cosine, cosine], axis=1).reshape(n, rp, HEAD_WIDTH)
    sin2 = jnp.concatenate([-sine, sine], axis=1).reshape(n, rp, HEAD_WIDTH)
    vmem = pl.BlockSpec(memory_space=pltpu.VMEM)
    smem = pl.BlockSpec(memory_space=pltpu.SMEM)
    hbm = pl.BlockSpec(memory_space=pl.ANY)
    V = pltpu.VMEM

    def sems(*shape):
        return [pltpu.SemaphoreType.DMA(shape)] * 2

    scratch = [
        V(w_query.shape, BF16), V(key_matrix.shape, BF16), V(value_matrix.shape, BF16),
        V(w_out.shape, BF16), V(w_gate.shape, BF16), V(w_up.shape, BF16),
        V((w_down.shape[0] - split, w_down.shape[1]), BF16), V(kv_cache.shape, BF16),
        V((total, cols), BF16), V((nh, rh, cols), F32),
        V((cq, n, rp, qc), F32), V((cq, n - 1, rp, qc), F32),
        V((n, rp, 2 * kw), F32), V((n - 1, rp, 2 * kw), F32),
        V((cq, n, rp, qc), BF16), V((n, rp, 2 * kw), BF16),
        V((kvl, per, total, HEAD_WIDTH), F32),
        V((kvl, total, HEAD_WIDTH), F32), V((kvl, total, HEAD_WIDTH), F32),
        V((n, kvl, per + 1, rp, HEAD_WIDTH), F32), V((n - 1, kvl, per + 1, rp, HEAD_WIDTH), F32),
        V((n, rp, qw), BF16), V((total, qw), BF16),
        V((co, nh, rh, oc), F32), V((co, nh - 1, rh, oc), F32),
        V((co, nh, rh, oc), BF16), V((total, ow), BF16),
        V((n, rp, HEAD_WIDTH), F32), V((n - 1, rp, HEAD_WIDTH), F32),
        V((rp, HEAD_WIDTH), F32),
        V((cg, n, 2, rp, gc), F32), V((cg, n - 1, 2, rp, gc), F32),
        V((cg, n, rp, gc), BF16), V((total, fw), BF16),
        V((co, nh, rh, oc), F32), V((co, nh - 1, rh, oc), F32),
        pltpu.SemaphoreType.DMA((cq,)), pltpu.SemaphoreType.DMA((4,)),
        pltpu.SemaphoreType.DMA((2, cg)), pltpu.SemaphoreType.DMA((2,)),
        *sems(cq, n - 1), *sems(n - 1), *sems(cq, n - 1), *sems(n - 1), *sems(n - 1), *sems(n - 1),
        *sems(co, nh - 1), *sems(co, nh - 1), *sems(n - 1), *sems(cg, n - 1),
        *sems(cg, n - 1), *sems(co, nh - 1),
    ]
    return pl.pallas_call(
        functools.partial(layer_kernel, n, nh, cq, co, cg, split),
        out_shape=jax.ShapeDtypeStruct((rh, ow), BF16),
        in_specs=[smem, smem] + [vmem] * 5 + [hbm] * 8,
        out_specs=vmem,
        scratch_shapes=scratch,
        compiler_params=pltpu.CompilerParams(
            collective_id=0, has_side_effects=True, vmem_limit_bytes=67043328
        ),
    )(
        slots, lengths, tokens, attn_gain.astype(F32)[None, :], ffn_gain.astype(F32)[None, :], cos2, sin2,
        w_query, key_matrix, value_matrix, w_out, w_gate, w_up, w_down, kv_cache,
    )


def solution(mesh):
    in_specs = (
        P("grp", None),
        P(),
        P("wide"),
        P("wide", "head"),
        P("wide", "head"),
        P("wide", "head"),
        P("head", "wide"),
        P("wide", "head"),
        P("wide", "head"),
        P("head", "wide"),
        P(None, "grp", "wide", "head"),
        P("grp"),
        P("grp"),
    )
    return jax.shard_map(
        functools.partial(per_device, mesh.shape["wide"], mesh.shape["head"]),
        mesh=mesh, in_specs=in_specs, out_specs=P(("grp", "head"), "wide"), check_vma=False,
    )
```
